32 devices in a mesh: dp: 4 (over z), tensor: 4 (over y, x), seq: 2 (over core).
Axes of the slice: x: 2, y: 2, z: 4, core: 2. Of those that a mesh axis runs over, the one named last changes fastest.
Arguments:
- hidden: bfloat16 [1024, 4096], P(('dp', 'seq'), 'tensor'), may hold values from -6 to 6
- w_in: bfloat16 [4096, 512], P('tensor'), may hold values from -0.09375 to 0.09375
- embed: bfloat16 [1024, 512], replicated, may hold values from -16 to 16
- gain: float32 [512], replicated, may hold values from 0.1 to 1.9
- w_head: bfloat16 [512, 1024], replicated, may hold values from -2 to 2
- tokens: int32 [1024, 8], P(('dp', 'seq')), may hold values from 0 to 1023
- frame_mask: int32 [1024], P(('dp', 'seq')), may hold values from 0 to 1, as said below
Outputs:
- loss: float32 [], replicated
- grad_head: float32 [524288], P(('dp', 'tensor', 'seq'))
- grad_hidden: bfloat16 [1024, 4096], P(('dp', 'seq'), 'tensor')
The draws below stay inside these ranges and needn't reach their ends.
Inputs may be any that keep to these rules, and one draw needn't show every extreme that they name: `frame_mask`: frame 0 always counts.
All inputs are finite; a program needn't handle non-finite values.
Results may differ from the reference program's by a relative error of at most 0.015.
Values may be sent and summed in bfloat16 or wider, within the bound.
A program may use at most 64 MiB of HBM per device.

```python
import jax
import jax.numpy as jnp
from jax import lax

D = 4096
DD = 512
V = 1024
K = 8
FR_DEV = 32
FRAMES = 1024
N_TENSOR = 4


def draw_embed(key, part):
    base = jnp.clip(jax.random.normal(jax.random.fold_in(key, 1), (V, DD), jnp.float32), -6.0, 6.0)
    return base.astype(jnp.bfloat16)


def draw_w_head(key, part):
    base = jax.random.normal(jax.random.fold_in(key, 4), (DD, V), jnp.float32) * DD ** (-0.5)
    return base.astype(jnp.bfloat16)


def draw_frame_mask(key, part):
    place = jnp.arange(FRAMES, dtype=jnp.int32)
    levels = jax.random.randint(key, (FRAMES,), 0, 1000)
    limit = 300 + 600 * (place // max(FRAMES // 1000, 1)) // max(FRAMES // max(FRAMES // 1000, 1), 1)
    counted = (levels < limit).astype(jnp.int32)
    return counted.at[0].set(1)


def place_ends(values, own_key, least, high):
    spot = [jax.random.randint(jax.random.fold_in(own_key, axis), (), 0, length) for axis, length in enumerate(values.shape)]
    widest = values.shape.index(max(values.shape))
    beside = spot[:widest] + [(spot[widest] + 1) % values.shape[widest]] + spot[widest + 1:]
    return values.at[tuple(spot)].set(least).at[tuple(beside)].set(high)


def shard_levels(stream_key, shape, cuts, low, high):
    def one(position, parts):
        draws = jax.random.uniform(jax.random.fold_in(jax.random.fold_in(stream_key, 6), position), (parts,), jnp.float32, low / len(cuts), high / len(cuts))
        return jnp.repeat(jnp.exp(draws), shape[position] // parts).reshape((-1,) + (1,) * (len(shape) - position - 1))

    factor_of = one(*cuts[0])
    for cut in cuts[1:]:
        factor_of = factor_of * one(*cut)
    return factor_of


def bell_draw(rng, dims, scale, reach, shards=(), kind=jnp.bfloat16):
    entries = scale * jax.random.normal(rng, dims, jnp.float32)
    if shards:
        entries = entries * shard_levels(rng, dims, shards, -0.22, 0.18)
    return jnp.clip(entries, -reach, reach).astype(kind)


def setup_inputs(seed: int = 0) -> dict:
    key_list = jax.random.split(jax.random.key(seed), 8)
    hidden = bell_draw(key_list[0], (FRAMES, D), 1.0, 6.0, ((0, 8), (1, 4)))
    w_in = bell_draw(key_list[1], (D, DD), D ** -0.5, 0.09375, ((0, 4),))
    embed = draw_embed(jax.random.fold_in(key_list[7], 71), 0)
    gain = jnp.clip(1.0 + 0.18 * jax.random.normal(key_list[3], (DD,), jnp.float32), 0.1, 1.9)
    w_head = draw_w_head(jax.random.fold_in(key_list[7], 71), 0)
    tokens = place_ends(jax.random.randint(key_list[5], (FRAMES, K), 0, V), jax.random.fold_in(key_list[5], 1), 0, V - 1).astype(jnp.int32)
    frame_mask = draw_frame_mask(jax.random.fold_in(key_list[7], 71), 0)
    return dict(hidden=hidden, w_in=w_in, embed=embed, gain=gain, w_head=w_head, tokens=tokens, frame_mask=frame_mask)


def block_terms(hblk, tblk, mblk, w_in, embed, gain, w_head, count):
    context = jnp.dot(hblk, w_in, preferred_element_type=jnp.float32).astype(jnp.bfloat16)
    frames = context.shape[0]
    width = context.shape[1]
    steps = tblk.shape[1]
    before = embed[tblk[:, :-1]].astype(jnp.float32)
    leading = jnp.zeros((frames, 1, width), jnp.float32)
    inputs = context.astype(jnp.float32)[:, None, :] + jnp.concatenate([leading, before], 1)
    inverse = lax.rsqrt(lax.optimization_barrier(jnp.mean(inputs * inputs, -1, keepdims=True)) + 1e-06)
    normed = inputs * inverse
    scaled = (normed * gain).astype(jnp.bfloat16)
    flat = scaled.reshape(frames * steps, width)
    logits = jnp.dot(flat, w_head, preferred_element_type=jnp.float32)
    top = lax.optimization_barrier(jnp.max(logits, -1, keepdims=True))
    total = top[:, 0] + jnp.log(lax.optimization_barrier(jnp.sum(jnp.exp(logits - top), -1)))
    target = tblk.reshape(-1)
    onehot = (target[:, None] == jnp.arange(w_head.shape[1], dtype=jnp.int32)[None, :]).astype(jnp.float32)
    nll = total - lax.optimization_barrier(jnp.sum(logits * onehot, -1))
    weights = (mblk.astype(jnp.float32)[:, None] * jnp.ones((1, steps), jnp.float32)).reshape(-1)
    loss_part = jnp.sum(weights * nll)
    probs = jnp.exp(logits - total[:, None])
    grad_logits = ((probs - onehot) * weights[:, None] / count).astype(jnp.bfloat16)
    head_term = lax.dot_general(flat, grad_logits, (((0,), (0,)), ((), ())), preferred_element_type=jnp.float32)
    grad_scaled = lax.dot_general(grad_logits, w_head, (((1,), (1,)), ((), ())), preferred_element_type=jnp.float32)
    scaled_grad = grad_scaled.reshape(inputs.shape) * gain
    grad_inputs = inverse * (scaled_grad - normed * lax.optimization_barrier(jnp.mean(scaled_grad * normed, -1, keepdims=True)))
    grad_context = lax.optimization_barrier(jnp.sum(grad_inputs, 1)).astype(jnp.bfloat16)
    return (loss_part, head_term, grad_context)

def reference(hidden, w_in, embed, gain, w_head, tokens, frame_mask):
    count = K * jnp.sum(frame_mask.astype(jnp.float32))
    block = N_TENSOR * FR_DEV
    blocks = hidden.shape[0] // block

    def advance(carry, pieces):
        loss_sum, head = carry
        hblk, tblk, mblk = pieces
        loss_part, head_term, grad_context = block_terms(hblk, tblk, mblk, w_in, embed, gain, w_head, count)
        grad_h = lax.dot_general(grad_context, w_in, (((1,), (1,)), ((), ())), preferred_element_type=jnp.float32).astype(jnp.bfloat16)
        return ((loss_sum + loss_part, head + head_term), grad_h)
    start = (jnp.zeros((), jnp.float32), jnp.zeros((w_head.shape[0], w_head.shape[1]), jnp.float32))
    pieces = (hidden.reshape(blocks, block, hidden.shape[1]), tokens.reshape(blocks, block, tokens.shape[1]), frame_mask.reshape(blocks, block))
    (loss_sum, head), grad_h = lax.scan(advance, start, pieces)
    return (loss_sum / count, head.reshape(-1), grad_h.reshape(hidden.shape))
```

```python
import functools

import jax
import jax.numpy as jnp
from jax import lax
from jax.experimental import pallas as pl
from jax.experimental.pallas import tpu as pltpu
from jax.sharding import PartitionSpec as P

F32 = jnp.float32
BF16 = jnp.bfloat16
MESH = pl.DeviceIdType.MESH
KCH = 2
GCAT = 3


def decode_terms(context, tok_rows, mask_rows, embed, gain, w_head, count_fn):
    frames = context.shape[0]
    width = context.shape[1]
    steps = tok_rows.shape[1]
    before = embed[tok_rows[:, :-1]].astype(jnp.float32)
    leading = jnp.zeros((frames, 1, width), jnp.float32)
    inputs = context.astype(jnp.float32)[:, None, :] + jnp.concatenate([leading, before], 1)
    inverse = lax.rsqrt(jnp.mean(inputs * inputs, -1, keepdims=True) + 1e-06)
    normed = inputs * inverse
    scaled = (normed * gain).astype(jnp.bfloat16)
    flat = scaled.reshape(frames * steps, width)
    logits = jnp.dot(flat, w_head, preferred_element_type=jnp.float32)
    top = jnp.max(logits, -1, keepdims=True)
    total = top[:, 0] + jnp.log(jnp.sum(jnp.exp(logits - top), -1))
    target = tok_rows.reshape(-1)
    onehot = (target[:, None] == jnp.arange(w_head.shape[1], dtype=jnp.int32)[None, :]).astype(
        jnp.float32
    )
    nll = total - jnp.sum(logits * onehot, -1)
    weights = (mask_rows.astype(jnp.float32)[:, None] * jnp.ones((1, steps), jnp.float32)).reshape(
        -1
    )
    count, loss_sum = count_fn(
        steps * jnp.sum(mask_rows.astype(jnp.float32)), jnp.sum(weights * nll)
    )
    probs = jnp.exp(logits - total[:, None])
    grad_logits = ((probs - onehot) * weights[:, None] / count).astype(jnp.bfloat16)
    head_term = lax.dot_general(
        flat, grad_logits, (((0,), (0,)), ((), ())), preferred_element_type=jnp.float32
    )
    grad_scaled = lax.dot_general(
        grad_logits, w_head, (((1,), (1,)), ((), ())), preferred_element_type=jnp.float32
    )
    scaled_grad = grad_scaled.reshape(inputs.shape) * gain
    grad_inputs = inverse * (
        scaled_grad - normed * jnp.mean(scaled_grad * normed, -1, keepdims=True)
    )
    grad_context = jnp.sum(grad_inputs, 1).astype(jnp.bfloat16)
    return (loss_sum / count, head_term, grad_context)


def add_totals(count_local, loss_local):
    return lax.psum((count_local, loss_local), ("dp", "tensor", "seq"))


def per_device_plain(hidden, w_in, embed, gain, w_head, tokens, frame_mask):
    groups = lax.axis_size("tensor")
    rows = hidden.shape[0] // groups
    context = lax.psum_scatter(
        jnp.dot(hidden, w_in, preferred_element_type=jnp.float32),
        "tensor",
        scatter_dimension=0,
        tiled=True,
    ).astype(jnp.bfloat16)
    offset = lax.axis_index("tensor") * rows
    tok_rows = lax.dynamic_slice_in_dim(tokens, offset, rows, 0)
    mask_rows = lax.dynamic_slice_in_dim(frame_mask, offset, rows, 0)
    loss, head_term, grad_context = decode_terms(
        context, tok_rows, mask_rows, embed, gain, w_head, add_totals
    )
    flat_term = head_term.reshape(-1)
    partial_grad = lax.psum_scatter(
        flat_term.astype(jnp.bfloat16), "dp", scatter_dimension=0, tiled=True
    ).astype(jnp.float32)
    grad_head = lax.psum_scatter(partial_grad, ("tensor", "seq"), scatter_dimension=0, tiled=True)
    product = lax.dot_general(
        lax.all_gather(grad_context, "tensor", axis=0, tiled=True),
        w_in,
        (((1,), (1,)), ((), ())),
        preferred_element_type=jnp.float32,
    )
    grad_hidden = product.astype(jnp.bfloat16)
    return (loss, grad_head, grad_hidden)


def kernel(
    sizes, hidden_h, w_in_h, embed_h, gain_h, w_head_h, tokens_h, mask_h,
    loss_o, head_o, gh_o,
    hidden, w_in, embed, gain, w_head, tokens, mask,
    ctx_own, ctx_send, ctx_recv, gath, scaled, gl, hs, r1, s1, r2, s2, r3, own,
    gc, st1, st1_r, st2, st2_r,
    in_sem, ctx_ss, ctx_rs, gc_ss, gc_rs,
    h1_ss, h1_rs, h2_ss, h2_rs, h3_ss, h3_rs, st1_ss, st1_rs, st2_ss, st2_rs,
):
    DP, T, S = sizes
    a, t, s = lax.axis_index("dp"), lax.axis_index("tensor"), lax.axis_index("seq")
    steps, nframes = tokens.shape
    frames = nframes // T
    feats = hidden.shape[1]
    width, vocab = w_head.shape
    rows = frames * steps
    piece = width // (DP * T * S)

    TX = 2 if T % 2 == 0 else 1
    TY = T // TX
    ty, tx = t // TX, lax.rem(t, TX)
    moves = sorted(
        [(dy, dx) for dy in range(TY) for dx in range(TX) if dy or dx],
        key=lambda m: -(m[0] > 0) - (m[1] > 0),
    )
    places = [lax.rem(ty + dy, TY) * TX + lax.rem(tx + dx, TX) for dy, dx in moves]

    barrier = pltpu.get_barrier_semaphore()
    peers_t = [{"tensor": p} for p in places]
    peers_p = [
        {"tensor": lax.rem(t + d, T), "seq": lax.rem(s + e, S)}
        for d in range(T)
        for e in range(S)
        if d or e
    ]
    peers_d = [{"dp": lax.rem(a + d, DP)} for d in range(1, DP)]
    for peer in peers_d + peers_p:
        pl.semaphore_signal(barrier, inc=1, device_id=peer, device_id_type=MESH)

    K = KCH
    part_k = feats // K
    pairs = []
    for i in range(K):
        at = pl.ds(i * part_k, part_k)
        pairs.append((hidden_h.at[:, at], hidden.at[:, at]))
        pairs.append((w_in_h.at[at, :], w_in.at[at, :]))
    pairs += [
        (tokens_h, tokens),
        (mask_h, mask),
        (embed_h, embed),
        (gain_h, gain),
        (w_head_h, w_head),
    ]
    loads = [
        pltpu.make_async_copy(src, dst, in_sem.at[i]) for i, (src, dst) in enumerate(pairs)
    ]
    for load in loads:
        load.start()
    rest = loads[2 * K :]

    sends = []

    def got(copy):
        copy.wait_recv()

    def send(src, dst, ss, rs, peer):
        copy = pltpu.make_async_remote_copy(
            src_ref=src, dst_ref=dst, send_sem=ss, recv_sem=rs, device_id=peer, device_id_type=MESH
        )
        copy.start()
        sends.append(copy)
        return copy

    part = None
    for i in range(K):
        loads[2 * i].wait()
        loads[2 * i + 1].wait()
        at = pl.ds(i * part_k, part_k)
        more = jnp.dot(hidden[:, at], w_in[at, :], preferred_element_type=F32)
        part = more if part is None else part + more
    part = part.reshape(T, frames, width)
    ctx_send[...] = part.astype(BF16)
    ctx_own[...] = part
    pl.semaphore_wait(barrier, len(peers_d) + len(peers_p))
    ctx_copies = [
        send(ctx_send.at[p], ctx_recv.at[i], ctx_ss.at[i], ctx_rs.at[i], peers_t[i])
        for i, p in enumerate(places)
    ]

    rest[0].wait()
    rest[1].wait()
    mask_row = mask[...].astype(F32)
    spot = lax.broadcasted_iota(jnp.int32, (frames, nframes), 0) + t * frames
    here = lax.broadcasted_iota(jnp.int32, (frames, nframes), 1)
    mine = spot == here
    tok = tokens[...].astype(F32)
    lanes = lax.broadcasted_iota(jnp.int32, (frames, vocab), 1).astype(F32)
    hot = [
        jnp.sum(jnp.where(mine, tok[k : k + 1, :], 0.0), 1, keepdims=True) == lanes
        for k in range(steps)
    ]
    rest[2].wait()
    prev = jnp.concatenate([jnp.where(h, 1.0, 0.0).astype(BF16) for h in hot[:-1]], 0)
    gath[...] = jnp.dot(prev, embed[...], preferred_element_type=F32)
    mcol = jnp.sum(jnp.where(mine, mask_row, 0.0), 1, keepdims=True)
    rest[3].wait()
    rest[4].wait()
    gvec = gain[...]

    ctx = ctx_own[t]
    for i in range(T - 1):
        got(ctx_copies[i])
        ctx = ctx + ctx_recv[i].astype(F32)
    ctx = ctx.astype(BF16).astype(F32)
    inputs = jnp.concatenate([ctx] * steps, 0) + jnp.concatenate(
        [jnp.zeros((frames, width), F32), gath[...]], 0
    )
    inverse = lax.rsqrt(jnp.mean(inputs * inputs, -1, keepdims=True) + 1e-06)
    normed = inputs * inverse
    flat = (normed * gvec).astype(BF16)
    scaled[...] = flat
    logits = jnp.dot(flat, w_head[...], preferred_element_type=F32)
    top = jnp.max(logits, -1, keepdims=True)
    powers = jnp.exp(logits - top)
    norm = jnp.sum(powers, -1, keepdims=True)
    onehot = jnp.concatenate([jnp.where(h, 1.0, 0.0) for h in hot], 0)
    weights = jnp.concatenate([mcol] * steps, 0)
    grads = ((powers * (1.0 / norm) - onehot) * weights).astype(BF16)
    gl[...] = grads

    chunk = width // DP
    h1, h2 = [], []

    def tensor_stage(j):
        acc = hs[j, :, s].astype(F32)
        for e in range(1, S):
            got(h1[j * (S - 1) + e - 1])
            acc = acc + r1[j, e - 1].astype(F32)
        s1[j] = acc.astype(BF16)
        for i, p in enumerate(places):
            h2.append(
                send(s1.at[j, p], r2.at[j, i], h2_ss.at[j, i], h2_rs.at[j, i], peers_t[i])
            )

    for j in range(DP):
        term = lax.dot_general(
            scaled[:, j * chunk : (j + 1) * chunk], gl[...], (((0,), (0,)), ((), ())),
            preferred_element_type=F32,
        )
        hs[j] = term.astype(BF16).reshape(T, S, piece, vocab)
        for e in range(1, S):
            h1.append(
                send(hs.at[j, :, lax.rem(s + e, S)], r1.at[j, e - 1], h1_ss.at[j, e - 1],
                     h1_rs.at[j, e - 1], {"seq": lax.rem(s + e, S)})
            )

    total = top + jnp.log(norm)
    nll = total - jnp.sum(logits * onehot, -1, keepdims=True)
    left = lax.broadcasted_iota(jnp.int32, st1.shape, 1) < st1.shape[1] // 2
    st1[...] = jnp.where(left, jnp.sum(weights * nll), jnp.sum(weights))
    stat1 = [
        send(st1, st1_r.at[i], st1_ss.at[i], st1_rs.at[i], peer) for i, peer in enumerate(peers_p)
    ]

    gc_copies = []

    def context_grad():
        grad_scaled = lax.dot_general(
            gl[...], w_head[...], (((1,), (1,)), ((), ())), preferred_element_type=F32
        )
        g = grad_scaled * gvec
        gi = inverse * (g - normed * jnp.mean(g * normed, -1, keepdims=True))
        gsum = gi[0:frames]
        for k in range(1, steps):
            gsum = gsum + gi[k * frames : (k + 1) * frames]
        gc[t] = gsum.astype(BF16)
        for i in range(T - 1):
            gc_copies.append(
                send(gc.at[t], gc.at[t], gc_ss.at[i], gc_rs.at[i], peers_t[i])
            )

    for j in range(DP):
        tensor_stage(j)
        if j == min(GCAT, DP - 1):
            context_grad()

    stats = st1[...]
    for i in range(len(peers_p)):
        got(stat1[i])
        stats = stats + st1_r[i]
    st2[...] = stats
    stat2 = [
        send(st2, st2_r.at[i], st2_ss.at[i], st2_rs.at[i], peer) for i, peer in enumerate(peers_d)
    ]

    def passes(j, slot, src):
        return pltpu.make_async_remote_copy(
            src_ref=src, dst_ref=r3.at[slot], send_sem=h3_ss.at[j], recv_sem=h3_rs.at[slot],
            device_id={"dp": j}, device_id_type=MESH,
        )

    for j in range(DP):
        acc = s1[j, t].astype(F32)
        for i in range(T - 1):
            got(h2[j * (T - 1) + i])
            acc = acc + r2[j, i].astype(F32)

        @pl.when(a == j)
        def _():
            own[...] = acc

        @pl.when(a != j)
        def _():
            s2[j] = acc.astype(BF16)
            passes(j, lax.rem(j - a + DP, DP) - 1, s2.at[j]).start()

    for i in range(DP - 1):
        got(stat2[i])
        stats = stats + st2_r[i]
    half = st1.shape[1] // 2
    share = 1.0 / stats[0:1, half : half + 1]
    for i in range(T - 1):
        got(gc_copies[i])
    product = lax.dot_general(
        gc[...].reshape(nframes, width), w_in[...], (((1,), (1,)), ((), ())),
        preferred_element_type=F32,
    )
    gh_o[...] = (product * share).astype(BF16)
    loss_o[...] = stats * share

    acc = own[...]
    for d in range(DP - 1):
        pltpu.make_async_remote_copy(
            src_ref=s2.at[d], dst_ref=r3.at[d], send_sem=h3_ss.at[d], recv_sem=h3_rs.at[d],
            device_id={"dp": lax.rem(a + 1, DP)}, device_id_type=MESH,
        ).wait_recv()
        acc = acc + r3[d].astype(F32)
    acc = acc * share
    groups = vocab // 128
    for b in range(groups):
        head_o[pl.ds(b, piece, stride=groups), :] = acc[:, b * 128 : (b + 1) * 128]
    for copy in sends:
        copy.wait_send()
    for j in range(DP):

        @pl.when(a != j)
        def _():
            passes(j, 0, s2.at[j]).wait_send()


def write_out(loss_i, head_i, gh_i, loss_o, head_o, gh_o, loss_v, sem):
    copies = [
        pltpu.make_async_copy(src, dst, sem.at[i])
        for i, (src, dst) in enumerate([(gh_i, gh_o), (head_i, head_o), (loss_v, loss_o)])
    ]
    copies[0].start()
    copies[1].start()
    loss_v[...] = loss_i[0:1, 0:1]
    copies[2].start()
    for copy in copies:
        copy.wait()


def per_device_kernel(hidden, w_in, embed, gain, w_head, tokens, frame_mask):
    DP, T, S = lax.axis_size("dp"), lax.axis_size("tensor"), lax.axis_size("seq")
    nframes, feats = hidden.shape
    steps = tokens.shape[1]
    frames = nframes // T
    width, vocab = w_head.shape
    rows = frames * steps
    piece = width // (DP * T * S)
    V = pltpu.VMEM
    dma = pltpu.SemaphoreType.DMA
    scratch = [
        V(hidden.shape, BF16), V(w_in.shape, BF16), V(embed.shape, BF16), V((1, width), F32),
        V(w_head.shape, BF16), V((steps, nframes), jnp.int32), V((1, nframes), jnp.int32),
        V((T, frames, width), F32),
        V((T, frames, width), BF16),
        V((T - 1, frames, width), BF16),
        V((rows - frames, width), F32),
        V((rows, width), BF16),
        V((rows, vocab), BF16),
        V((DP, T, S, piece, vocab), BF16),
        V((DP, S - 1, T, piece, vocab), BF16),
        V((DP, T, piece, vocab), BF16),
        V((DP, T - 1, piece, vocab), BF16),
        V((DP, piece, vocab), BF16),
        V((DP - 1, piece, vocab), BF16),
        V((piece, vocab), F32),
        V((T, frames, width), BF16),
        V((8, 128), F32), V((T * S - 1, 8, 128), F32),
        V((8, 128), F32), V((DP - 1, 8, 128), F32),
        dma((2 * KCH + 5,)),
        dma((T - 1,)), dma((T - 1,)), dma((T - 1,)), dma((T - 1,)),
        dma((DP, S - 1)), dma((DP, S - 1)), dma((DP, T - 1)), dma((DP, T - 1)),
        dma((DP,)), dma((DP - 1,)),
        dma((T * S - 1,)), dma((T * S - 1,)), dma((DP - 1,)), dma((DP - 1,)),
    ]
    head_shape = jax.ShapeDtypeStruct((piece * vocab // 128, 128), F32)
    gh_shape = jax.ShapeDtypeStruct((nframes, feats), BF16)
    vmem = pl.BlockSpec(memory_space=pltpu.VMEM)
    results = pl.pallas_call(
        functools.partial(kernel, (DP, T, S)),
        out_shape=(jax.ShapeDtypeStruct((8, 128), F32), head_shape, gh_shape),
        in_specs=[pl.BlockSpec(memory_space=pltpu.HBM)] * 7,
        out_specs=(vmem, vmem, vmem),
        scratch_shapes=scratch,
        compiler_params=pltpu.CompilerParams(
            collective_id=0, has_side_effects=True, vmem_limit_bytes=40 << 20
        ),
        name="decode",
    )(*[pltpu.with_memory_space_constraint(x, pltpu.HBM) for x in (hidden, w_in, embed, gain.reshape(1, -1), w_head, tokens.T, frame_mask.reshape(1, -1))])
    loss, head, grad_hidden = pl.pallas_call(
        write_out,
        out_shape=(jax.ShapeDtypeStruct((1, 1), F32), head_shape, gh_shape),
        in_specs=[vmem] + [pl.BlockSpec(memory_space=pl.ANY)] * 2,
        out_specs=(pl.BlockSpec(memory_space=pltpu.HBM),) * 3,
        scratch_shapes=[V((1, 1), F32), dma((3,))],
        compiler_params=pltpu.CompilerParams(vmem_limit_bytes=4 << 20),
        name="write_out",
    )(*results)
    return loss.reshape(()), head.reshape(-1), grad_hidden


def solution(mesh):
    def per_device(hidden, w_in, embed, gain, w_head, tokens, frame_mask):
        DP, T, S = mesh.shape["dp"], mesh.shape["tensor"], mesh.shape["seq"]
        width, vocab = w_head.shape
        fits = (
            width % (16 * DP * T * S) == 0
            and width % (128 * DP) == 0
            and vocab % 128 == 0
            and hidden.shape[0] % (16 * T) == 0
            and min(DP, T, S) > 1
        )
        run = per_device_kernel if fits else per_device_plain
        return run(hidden, w_in, embed, gain, w_head, tokens, frame_mask)

    placed = (
        P(("dp", "seq"), "tensor"),
        P("tensor", None),
        P(),
        P(),
        P(),
        P(("dp", "seq"), None),
        P(("dp", "seq")),
    )
    return jax.shard_map(
        per_device,
        mesh=mesh,
        in_specs=placed,
        out_specs=(P(), P(("dp", "tensor", "seq")), P(("dp", "seq"), "tensor")),
        check_vma=False,
    )
```

```python
import functools

import jax
import jax.numpy as jnp
from jax import lax
from jax.experimental import pallas as pl
from jax.experimental.pallas import tpu as pltpu
from jax.sharding import PartitionSpec as P

F32 = jnp.float32
BF16 = jnp.bfloat16
MESH = pl.DeviceIdType.MESH
KCH = 2
PAIR = 2
GCAT = 3
STAT = -1
LAT = 0
EARLY = 2
ZAT = 2
ZSHARE = 3


def decode_terms(context, tok_rows, mask_rows, embed, gain, w_head, count_fn):
    frames = context.shape[0]
    width = context.shape[1]
    steps = tok_rows.shape[1]
    before = embed[tok_rows[:, :-1]].astype(jnp.float32)
    leading = jnp.zeros((frames, 1, width), jnp.float32)
    inputs = context.astype(jnp.float32)[:, None, :] + jnp.concatenate([leading, before], 1)
    inverse = lax.rsqrt(jnp.mean(inputs * inputs, -1, keepdims=True) + 1e-06)
    normed = inputs * inverse
    scaled = (normed * gain).astype(jnp.bfloat16)
    flat = scaled.reshape(frames * steps, width)
    logits = jnp.dot(flat, w_head, preferred_element_type=jnp.float32)
    top = jnp.max(logits, -1, keepdims=True)
    total = top[:, 0] + jnp.log(jnp.sum(jnp.exp(logits - top), -1))
    target = tok_rows.reshape(-1)
    onehot = (target[:, None] == jnp.arange(w_head.shape[1], dtype=jnp.int32)[None, :]).astype(
        jnp.float32
    )
    nll = total - jnp.sum(logits * onehot, -1)
    weights = (mask_rows.astype(jnp.float32)[:, None] * jnp.ones((1, steps), jnp.float32)).reshape(
        -1
    )
    count, loss_sum = count_fn(
        steps * jnp.sum(mask_rows.astype(jnp.float32)), jnp.sum(weights * nll)
    )
    probs = jnp.exp(logits - total[:, None])
    grad_logits = ((probs - onehot) * weights[:, None] / count).astype(jnp.bfloat16)
    head_term = lax.dot_general(
        flat, grad_logits, (((0,), (0,)), ((), ())), preferred_element_type=jnp.float32
    )
    grad_scaled = lax.dot_general(
        grad_logits, w_head, (((1,), (1,)), ((), ())), preferred_element_type=jnp.float32
    )
    scaled_grad = grad_scaled.reshape(inputs.shape) * gain
    grad_inputs = inverse * (
        scaled_grad - normed * jnp.mean(scaled_grad * normed, -1, keepdims=True)
    )
    grad_context = jnp.sum(grad_inputs, 1).astype(jnp.bfloat16)
    return (loss_sum / count, head_term, grad_context)


def add_totals(count_local, loss_local):
    return lax.psum((count_local, loss_local), ("dp", "tensor", "seq"))


def per_device_plain(hidden, w_in, embed, gain, w_head, tokens, frame_mask):
    groups = lax.axis_size("tensor")
    rows = hidden.shape[0] // groups
    context = lax.psum_scatter(
        jnp.dot(hidden, w_in, preferred_element_type=jnp.float32),
        "tensor",
        scatter_dimension=0,
        tiled=True,
    ).astype(jnp.bfloat16)
    offset = lax.axis_index("tensor") * rows
    tok_rows = lax.dynamic_slice_in_dim(tokens, offset, rows, 0)
    mask_rows = lax.dynamic_slice_in_dim(frame_mask, offset, rows, 0)
    loss, head_term, grad_context = decode_terms(
        context, tok_rows, mask_rows, embed, gain, w_head, add_totals
    )
    flat_term = head_term.reshape(-1)
    partial_grad = lax.psum_scatter(
        flat_term.astype(jnp.bfloat16), "dp", scatter_dimension=0, tiled=True
    ).astype(jnp.float32)
    grad_head = lax.psum_scatter(partial_grad, ("tensor", "seq"), scatter_dimension=0, tiled=True)
    product = lax.dot_general(
        lax.all_gather(grad_context, "tensor", axis=0, tiled=True),
        w_in,
        (((1,), (1,)), ((), ())),
        preferred_element_type=jnp.float32,
    )
    grad_hidden = product.astype(jnp.bfloat16)
    return (loss, grad_head, grad_hidden)


def kernel(
    sizes, hidden_h, w_in_h, embed_h, gain_h, w_head_h, tokens_h, mask_h,
    loss_o, head_o, gh_o,
    hidden, w_in, embed, gain, w_head, tokens, mask,
    ctx_own, ctx_send, ctx_recv, gath, scaled, gl, hs, r1, s1, r2, s2, r3, own,
    z1, rz, zown, z2, rz2, gc, st1, st1_r, st2, st2_r,
    in_sem, ctx_ss, ctx_rs, gc_ss, gc_rs,
    h1_ss, h1_rs, h2_ss, h2_rs, h3_ss, h3_rs, z1_ss, z1_rs, z2_ss, z2_rs,
    st1_ss, st1_rs, st2_ss, st2_rs,
):
    DP, T, S = sizes
    a, t, s = lax.axis_index("dp"), lax.axis_index("tensor"), lax.axis_index("seq")
    steps, nframes = tokens.shape
    frames = nframes // T
    feats = hidden.shape[1]
    width, vocab = w_head.shape
    rows = frames * steps
    piece = width // (DP * T * S)

    TX = 2 if T % 2 == 0 else 1
    TY = T // TX
    ty, tx = t // TX, lax.rem(t, TX)
    moves = sorted(
        [(dy, dx) for dy in range(TY) for dx in range(TX) if dy or dx],
        key=lambda m: -(m[0] > 0) - (m[1] > 0),
    )
    places = [lax.rem(ty + dy, TY) * TX + lax.rem(tx + dx, TX) for dy, dx in moves]

    barrier = pltpu.get_barrier_semaphore()
    peers_t = [{"tensor": p} for p in places]
    peers_p = [
        {"tensor": lax.rem(t + d, T), "seq": lax.rem(s + e, S)}
        for d in range(T)
        for e in range(S)
        if d or e
    ]
    peers_d = [{"dp": lax.rem(a + d, DP)} for d in range(1, DP)]
    for peer in peers_d + peers_p:
        pl.semaphore_signal(barrier, inc=1, device_id=peer, device_id_type=MESH)

    K = KCH
    part_k = feats // K
    pairs = []
    for i in range(K):
        at = pl.ds(i * part_k, part_k)
        pairs.append((hidden_h.at[:, at], hidden.at[:, at]))
        pairs.append((w_in_h.at[at, :], w_in.at[at, :]))
    pairs += [
        (tokens_h, tokens),
        (mask_h, mask),
        (embed_h, embed),
        (gain_h, gain),
        (w_head_h, w_head),
    ]
    loads = [
        pltpu.make_async_copy(src, dst, in_sem.at[i]) for i, (src, dst) in enumerate(pairs)
    ]
    rest = loads[2 * K :]
    for load in loads[: 2 * K] + rest[:EARLY]:
        load.start()

    sends = []

    def got(copy):
        copy.wait_recv()

    def send(src, dst, ss, rs, peer):
        copy = pltpu.make_async_remote_copy(
            src_ref=src, dst_ref=dst, send_sem=ss, recv_sem=rs, device_id=peer, device_id_type=MESH
        )
        copy.start()
        sends.append(copy)
        return copy

    part = None
    for i in range(K):
        loads[2 * i].wait()
        loads[2 * i + 1].wait()
        at = pl.ds(i * part_k, part_k)
        more = jnp.dot(hidden[:, at], w_in[at, :], preferred_element_type=F32)
        part = more if part is None else part + more
        if i == 0:
            for load in rest[EARLY:]:
                load.start()
    part = part.reshape(T, frames, width)
    ctx_send[...] = part.astype(BF16)
    ctx_own[...] = part
    pl.semaphore_wait(barrier, len(peers_d) + len(peers_p))
    ctx_copies = [
        send(ctx_send.at[p], ctx_recv.at[i], ctx_ss.at[i], ctx_rs.at[i], peers_t[i])
        for i, p in enumerate(places)
    ]

    rest[0].wait()
    rest[1].wait()
    mask_row = mask[...].astype(F32)
    spot = lax.broadcasted_iota(jnp.int32, (frames, nframes), 0) + t * frames
    here = lax.broadcasted_iota(jnp.int32, (frames, nframes), 1)
    mine = spot == here
    tok = tokens[...].astype(F32)
    lanes = lax.broadcasted_iota(jnp.int32, (frames, vocab), 1).astype(F32)
    hot = [
        jnp.sum(jnp.where(mine, tok[k : k + 1, :], 0.0), 1, keepdims=True) == lanes
        for k in range(steps)
    ]
    rest[2].wait()
    prev = jnp.concatenate([jnp.where(h, 1.0, 0.0).astype(BF16) for h in hot[:-1]], 0)
    gath[...] = jnp.dot(prev, embed[...], preferred_element_type=F32)
    mcol = jnp.sum(jnp.where(mine, mask_row, 0.0), 1, keepdims=True)
    rest[3].wait()
    rest[4].wait()
    gvec = gain[...]

    ctx = ctx_own[t]
    for i in range(T - 1):
        got(ctx_copies[i])
        ctx = ctx + ctx_recv[i].astype(F32)
    ctx = ctx.astype(BF16).astype(F32)
    inputs = jnp.concatenate([ctx] * steps, 0) + jnp.concatenate(
        [jnp.zeros((frames, width), F32), gath[...]], 0
    )
    inverse = lax.rsqrt(jnp.mean(inputs * inputs, -1, keepdims=True) + 1e-06)
    normed = inputs * inverse
    flat = (normed * gvec).astype(BF16)
    scaled[...] = flat
    logits = jnp.dot(flat, w_head[...], preferred_element_type=F32)
    top = jnp.max(logits, -1, keepdims=True)
    powers = jnp.exp(logits - top)
    norm = jnp.sum(powers, -1, keepdims=True)
    onehot = jnp.concatenate([jnp.where(h, 1.0, 0.0) for h in hot], 0)
    weights = jnp.concatenate([mcol] * steps, 0)
    grads = ((powers * (1.0 / norm) - onehot) * weights).astype(BF16)
    gl[...] = grads

    chunk = width // DP
    h1, h2 = [], []

    cut = s1.shape[3]

    def along_dp(j, slot, src, dst, ss, rs):
        return pltpu.make_async_remote_copy(
            src_ref=src, dst_ref=dst.at[slot], send_sem=ss.at[j], recv_sem=rs.at[slot],
            device_id={"dp": j}, device_id_type=MESH,
        )

    def tensor_stage(j):
        acc = hs[j, :, s].astype(F32)
        for e in range(1, S):
            got(h1[j * (S - 1) + e - 1])
            acc = acc + r1[j, e - 1].astype(F32)
        s1[j] = acc[:, :, :cut].astype(BF16)
        for i, p in enumerate(places):
            h2.append(
                send(s1.at[j, p], r2.at[j, i], h2_ss.at[j, i], h2_rs.at[j, i], peers_t[i])
            )

        z1[j] = acc[:, :, cut:].astype(BF16)

        @pl.when(a != j)
        def _():
            along_dp(j, lax.rem(j - a + DP, DP) - 1, z1.at[j], rz, z1_ss, z1_rs).start()

    for j0 in range(0, DP, PAIR):
        term = lax.dot_general(
            scaled[:, j0 * chunk : (j0 + PAIR) * chunk], gl[...], (((0,), (0,)), ((), ())),
            preferred_element_type=F32,
        )
        for j in range(j0, j0 + PAIR):
            hs[j] = term[(j - j0) * chunk : (j - j0 + 1) * chunk].astype(BF16).reshape(
                T, S, piece, vocab
            )
            for e in range(1, S):
                h1.append(
                    send(hs.at[j, :, lax.rem(s + e, S)], r1.at[j, e - 1], h1_ss.at[j, e - 1],
                         h1_rs.at[j, e - 1], {"seq": lax.rem(s + e, S)})
                )

    stat1, stat2 = [], []

    def statistics():
        total = top + jnp.log(norm)
        nll = total - jnp.sum(logits * onehot, -1, keepdims=True)
        left = lax.broadcasted_iota(jnp.int32, st1.shape, 1) < st1.shape[1] // 2
        st1[...] = jnp.where(left, jnp.sum(weights * nll), jnp.sum(weights))
        for i, peer in enumerate(peers_p):
            stat1.append(send(st1, st1_r.at[i], st1_ss.at[i], st1_rs.at[i], peer))

    gc_copies = []

    def context_grad():
        grad_scaled = lax.dot_general(
            gl[...], w_head[...], (((1,), (1,)), ((), ())), preferred_element_type=F32
        )
        g = grad_scaled * gvec
        gi = inverse * (g - normed * jnp.mean(g * normed, -1, keepdims=True))
        gsum = gi[0:frames]
        for k in range(1, steps):
            gsum = gsum + gi[k * frames : (k + 1) * frames]
        gc[t] = gsum.astype(BF16)
        for i in range(T - 1):
            gc_copies.append(
                send(gc.at[t], gc.at[t], gc_ss.at[i], gc_rs.at[i], peers_t[i])
            )

    if STAT < 0:
        statistics()
    for j in range(DP):
        tensor_stage(j)
        if j == min(STAT, DP - 1):
            statistics()
        if j == min(GCAT, DP - 1):
            context_grad()

    z2c = []

    def z_stage():
        acc = jnp.zeros(zown.shape, F32)
        for j in range(DP):
            acc = acc + jnp.where(a == j, z1[j].astype(F32), 0.0)
        for d in range(DP - 1):
            along_dp(d, d, z1.at[d], rz, z1_ss, z1_rs).wait_recv()
            acc = acc + rz[d].astype(F32)
        z2[...] = acc.astype(BF16)
        zown[...] = acc
        for i, p in enumerate(places):
            z2c.append(send(z2.at[p], rz2.at[i], z2_ss.at[i], z2_rs.at[i], peers_t[i]))

    for j in range(DP):
        if j == min(LAT, DP - 1):
            stats = st1[...]
            for i in range(len(peers_p)):
                got(stat1[i])
                stats = stats + st1_r[i]
            st2[...] = stats
            for i, peer in enumerate(peers_d):
                stat2.append(send(st2, st2_r.at[i], st2_ss.at[i], st2_rs.at[i], peer))
        acc = s1[j, t].astype(F32)
        for i in range(T - 1):
            got(h2[j * (T - 1) + i])
            acc = acc + r2[j, i].astype(F32)

        @pl.when(a == j)
        def _():
            own[...] = acc

        @pl.when(a != j)
        def _():
            s2[j] = acc.astype(BF16)
            along_dp(j, lax.rem(j - a + DP, DP) - 1, s2.at[j], r3, h3_ss, h3_rs).start()

        if j == min(ZAT, DP - 1):
            z_stage()

    for i in range(DP - 1):
        got(stat2[i])
        stats = stats + st2_r[i]
    half = st1.shape[1] // 2
    share = 1.0 / stats[0:1, half : half + 1]
    for i in range(T - 1):
        got(gc_copies[i])
    product = lax.dot_general(
        gc[...].reshape(nframes, width), w_in[...], (((1,), (1,)), ((), ())),
        preferred_element_type=F32,
    )
    gh_o[...] = (product * share).astype(BF16)
    loss_o[...] = stats * share

    groups = vocab // 128
    low = cut // 128
    acc = zown[t]
    for i in range(T - 1):
        got(z2c[i])
        acc = acc + rz2[i].astype(F32)
    acc = acc * share
    for b in range(low, groups):
        head_o[pl.ds(b, piece, stride=groups), :] = acc[:, (b - low) * 128 : (b - low + 1) * 128]
    acc = own[...]
    for d in range(DP - 1):
        along_dp(d, d, s2.at[d], r3, h3_ss, h3_rs).wait_recv()
        acc = acc + r3[d].astype(F32)
    acc = acc * share
    for b in range(low):
        head_o[pl.ds(b, piece, stride=groups), :] = acc[:, b * 128 : (b + 1) * 128]
    for copy in sends:
        copy.wait_send()
    for j in range(DP):

        @pl.when(a != j)
        def _():
            along_dp(j, 0, z1.at[j], rz, z1_ss, z1_rs).wait_send()
            along_dp(j, 0, s2.at[j], r3, h3_ss, h3_rs).wait_send()


def write_out(loss_i, head_i, gh_i, loss_o, head_o, gh_o, loss_v, sem):
    copies = [
        pltpu.make_async_copy(src, dst, sem.at[i])
        for i, (src, dst) in enumerate([(gh_i, gh_o), (head_i, head_o), (loss_v, loss_o)])
    ]
    copies[0].start()
    copies[1].start()
    loss_v[...] = loss_i[0:1, 0:1]
    copies[2].start()
    for copy in copies:
        copy.wait()


def per_device_kernel(hidden, w_in, embed, gain, w_head, tokens, frame_mask):
    DP, T, S = lax.axis_size("dp"), lax.axis_size("tensor"), lax.axis_size("seq")
    nframes, feats = hidden.shape
    steps = tokens.shape[1]
    frames = nframes // T
    width, vocab = w_head.shape
    rows = frames * steps
    piece = width // (DP * T * S)
    tail = max(vocab // 128 * ZSHARE // 8, 1) * 128
    cut = vocab - tail
    V = pltpu.VMEM
    dma = pltpu.SemaphoreType.DMA
    scratch = [
        V(hidden.shape, BF16), V(w_in.shape, BF16), V(embed.shape, BF16), V((1, width), F32),
        V(w_head.shape, BF16), V((steps, nframes), jnp.int32), V((1, nframes), jnp.int32),
        V((T, frames, width), F32),
        V((T, frames, width), BF16),
        V((T - 1, frames, width), BF16),
        V((rows - frames, width), F32),
        V((rows, width), BF16),
        V((rows, vocab), BF16),
        V((DP, T, S, piece, vocab), BF16),
        V((DP, S - 1, T, piece, vocab), BF16),
        V((DP, T, piece, cut), BF16),
        V((DP, T - 1, piece, cut), BF16),
        V((DP, piece, cut), BF16),
        V((DP - 1, piece, cut), BF16),
        V((piece, cut), F32),
        V((DP, T, piece, tail), BF16),
        V((DP - 1, T, piece, tail), BF16),
        V((T, piece, tail), F32),
        V((T, piece, tail), BF16),
        V((T - 1, piece, tail), BF16),
        V((T, frames, width), BF16),
        V((8, 128), F32), V((T * S - 1, 8, 128), F32),
        V((8, 128), F32), V((DP - 1, 8, 128), F32),
        dma((2 * KCH + 5,)),
        dma((T - 1,)), dma((T - 1,)), dma((T - 1,)), dma((T - 1,)),
        dma((DP, S - 1)), dma((DP, S - 1)), dma((DP, T - 1)), dma((DP, T - 1)),
        dma((DP,)), dma((DP - 1,)), dma((DP,)), dma((DP - 1,)), dma((T - 1,)), dma((T - 1,)),
        dma((T * S - 1,)), dma((T * S - 1,)), dma((DP - 1,)), dma((DP - 1,)),
    ]
    head_shape = jax.ShapeDtypeStruct((piece * vocab // 128, 128), F32)
    gh_shape = jax.ShapeDtypeStruct((nframes, feats), BF16)
    vmem = pl.BlockSpec(memory_space=pltpu.VMEM)
    results = pl.pallas_call(
        functools.partial(kernel, (DP, T, S)),
        out_shape=(jax.ShapeDtypeStruct((8, 128), F32), head_shape, gh_shape),
        in_specs=[pl.BlockSpec(memory_space=pltpu.HBM)] * 7,
        out_specs=(vmem, vmem, vmem),
        scratch_shapes=scratch,
        compiler_params=pltpu.CompilerParams(
            collective_id=0, has_side_effects=True, vmem_limit_bytes=40 << 20
        ),
        name="decode",
    )(*[pltpu.with_memory_space_constraint(x, pltpu.HBM) for x in (hidden, w_in, embed, gain.reshape(1, -1), w_head, tokens.T, frame_mask.reshape(1, -1))])
    loss, head, grad_hidden = pl.pallas_call(
        write_out,
        out_shape=(jax.ShapeDtypeStruct((1, 1), F32), head_shape, gh_shape),
        in_specs=[vmem] + [pl.BlockSpec(memory_space=pl.ANY)] * 2,
        out_specs=(pl.BlockSpec(memory_space=pltpu.HBM),) * 3,
        scratch_shapes=[V((1, 1), F32), dma((3,))],
        compiler_params=pltpu.CompilerParams(vmem_limit_bytes=4 << 20),
        name="write_out",
    )(*results)
    return loss.reshape(()), head.reshape(-1), grad_hidden


def solution(mesh):
    def per_device(hidden, w_in, embed, gain, w_head, tokens, frame_mask):
        DP, T, S = mesh.shape["dp"], mesh.shape["tensor"], mesh.shape["seq"]
        width, vocab = w_head.shape
        fits = (
            width % (16 * DP * T * S) == 0
            and width % (128 * DP) == 0
            and vocab % 128 == 0
            and vocab > 128
            and hidden.shape[0] % (16 * T) == 0
            and min(DP, T, S) > 1
            and DP % PAIR == 0
        )
        run = per_device_kernel if fits else per_device_plain
        return run(hidden, w_in, embed, gain, w_head, tokens, frame_mask)

    placed = (
        P(("dp", "seq"), "tensor"),
        P("tensor", None),
        P(),
        P(),
        P(),
        P(("dp", "seq"), None),
        P(("dp", "seq")),
    )
    return jax.shard_map(
        per_device,
        mesh=mesh,
        in_specs=placed,
        out_specs=(P(), P(("dp", "tensor", "seq")), P(("dp", "seq"), "tensor")),
        check_vma=False,
    )
```

```python
import functools

import jax
import jax.numpy as jnp
from jax import lax
from jax.experimental import pallas as pl
from jax.experimental.pallas import tpu as pltpu
from jax.sharding import PartitionSpec as P

F32 = jnp.float32
BF16 = jnp.bfloat16
MESH = pl.DeviceIdType.MESH
KCH = 2
PAIR = 4
GCAT = 3
STAT = -1
LAT = 0
EARLY = 7
ZAT = 1
ZSHARE = 3


def decode_terms(context, tok_rows, mask_rows, embed, gain, w_head, count_fn):
    frames = context.shape[0]
    width = context.shape[1]
    steps = tok_rows.shape[1]
    before = embed[tok_rows[:, :-1]].astype(jnp.float32)
    leading = jnp.zeros((frames, 1, width), jnp.float32)
    inputs = context.astype(jnp.float32)[:, None, :] + jnp.concatenate([leading, before], 1)
    inverse = lax.rsqrt(jnp.mean(inputs * inputs, -1, keepdims=True) + 1e-06)
    normed = inputs * inverse
    scaled = (normed * gain).astype(jnp.bfloat16)
    flat = scaled.reshape(frames * steps, width)
    logits = jnp.dot(flat, w_head, preferred_element_type=jnp.float32)
    top = jnp.max(logits, -1, keepdims=True)
    total = top[:, 0] + jnp.log(jnp.sum(jnp.exp(logits - top), -1))
    target = tok_rows.reshape(-1)
    onehot = (target[:, None] == jnp.arange(w_head.shape[1], dtype=jnp.int32)[None, :]).astype(
        jnp.float32
    )
    nll = total - jnp.sum(logits * onehot, -1)
    weights = (mask_rows.astype(jnp.float32)[:, None] * jnp.ones((1, steps), jnp.float32)).reshape(
        -1
    )
    count, loss_sum = count_fn(
        steps * jnp.sum(mask_rows.astype(jnp.float32)), jnp.sum(weights * nll)
    )
    probs = jnp.exp(logits - total[:, None])
    grad_logits = ((probs - onehot) * weights[:, None] / count).astype(jnp.bfloat16)
    head_term = lax.dot_general(
        flat, grad_logits, (((0,), (0,)), ((), ())), preferred_element_type=jnp.float32
    )
    grad_scaled = lax.dot_general(
        grad_logits, w_head, (((1,), (1,)), ((), ())), preferred_element_type=jnp.float32
    )
    scaled_grad = grad_scaled.reshape(inputs.shape) * gain
    grad_inputs = inverse * (
        scaled_grad - normed * jnp.mean(scaled_grad * normed, -1, keepdims=True)
    )
    grad_context = jnp.sum(grad_inputs, 1).astype(jnp.bfloat16)
    return (loss_sum / count, head_term, grad_context)


def add_totals(count_local, loss_local):
    return lax.psum((count_local, loss_local), ("dp", "tensor", "seq"))


def per_device_plain(hidden, w_in, embed, gain, w_head, tokens, frame_mask):
    groups = lax.axis_size("tensor")
    rows = hidden.shape[0] // groups
    context = lax.psum_scatter(
        jnp.dot(hidden, w_in, preferred_element_type=jnp.float32),
        "tensor",
        scatter_dimension=0,
        tiled=True,
    ).astype(jnp.bfloat16)
    offset = lax.axis_index("tensor") * rows
    tok_rows = lax.dynamic_slice_in_dim(tokens, offset, rows, 0)
    mask_rows = lax.dynamic_slice_in_dim(frame_mask, offset, rows, 0)
    loss, head_term, grad_context = decode_terms(
        context, tok_rows, mask_rows, embed, gain, w_head, add_totals
    )
    flat_term = head_term.reshape(-1)
    partial_grad = lax.psum_scatter(
        flat_term.astype(jnp.bfloat16), "dp", scatter_dimension=0, tiled=True
    ).astype(jnp.float32)
    grad_head = lax.psum_scatter(partial_grad, ("tensor", "seq"), scatter_dimension=0, tiled=True)
    product = lax.dot_general(
        lax.all_gather(grad_context, "tensor", axis=0, tiled=True),
        w_in,
        (((1,), (1,)), ((), ())),
        preferred_element_type=jnp.float32,
    )
    grad_hidden = product.astype(jnp.bfloat16)
    return (loss, grad_head, grad_hidden)


def kernel(
    sizes, hidden_h, w_in_h, embed_h, gain_h, w_head_h, tokens_h, mask_h,
    loss_o, head_o, gh_o,
    hidden, w_in, embed, gain, w_head, tokens, mask,
    ctx_own, ctx_send, ctx_recv, gath, scaled, gl, hs, r1, s1, r2, s2, r3, own,
    z1, rz, zown, z2, rz2, gc, st1, st1_r, st2, st2_r,
    in_sem, ctx_ss, ctx_rs, gc_ss, gc_rs,
    h1_ss, h1_rs, h2_ss, h2_rs, h3_ss, h3_rs, z1_ss, z1_rs, z2_ss, z2_rs,
    st1_ss, st1_rs, st2_ss, st2_rs,
):
    DP, T, S = sizes
    a, t, s = lax.axis_index("dp"), lax.axis_index("tensor"), lax.axis_index("seq")
    steps, nframes = tokens.shape
    frames = nframes // T
    feats = hidden.shape[1]
    width, vocab = w_head.shape
    rows = frames * steps
    piece = width // (DP * T * S)

    TX = 2 if T % 2 == 0 else 1
    TY = T // TX
    ty, tx = t // TX, lax.rem(t, TX)
    moves = sorted(
        [(dy, dx) for dy in range(TY) for dx in range(TX) if dy or dx],
        key=lambda m: -(m[0] > 0) - (m[1] > 0),
    )
    places = [lax.rem(ty + dy, TY) * TX + lax.rem(tx + dx, TX) for dy, dx in moves]

    barrier = pltpu.get_barrier_semaphore()
    peers_t = [{"tensor": p} for p in places]
    peers_p = [
        {"tensor": lax.rem(t + d, T), "seq": lax.rem(s + e, S)}
        for d in range(T)
        for e in range(S)
        if d or e
    ]
    peers_d = [{"dp": lax.rem(a + d, DP)} for d in range(1, DP)]
    for peer in peers_d + peers_p:
        pl.semaphore_signal(barrier, inc=1, device_id=peer, device_id_type=MESH)

    K = KCH
    part_k = feats // K
    pairs = []
    for i in range(K):
        at = pl.ds(i * part_k, part_k)
        pairs.append((hidden_h.at[:, at], hidden.at[:, at]))
        pairs.append((w_in_h.at[at, :], w_in.at[at, :]))
    pairs += [
        (tokens_h, tokens),
        (mask_h, mask),
        (embed_h, embed),
        (gain_h, gain),
        (w_head_h, w_head),
    ]
    loads = [
        pltpu.make_async_copy(src, dst, in_sem.at[i]) for i, (src, dst) in enumerate(pairs)
    ]
    rest = loads[2 * K :]
    for load in loads[: 2 * K] + rest[:EARLY]:
        load.start()

    sends = []

    def got(copy):
        copy.wait_recv()

    def send(src, dst, ss, rs, peer):
        copy = pltpu.make_async_remote_copy(
            src_ref=src, dst_ref=dst, send_sem=ss, recv_sem=rs, device_id=peer, device_id_type=MESH
        )
        copy.start()
        sends.append(copy)
        return copy

    part = None
    for i in range(K):
        loads[2 * i].wait()
        loads[2 * i + 1].wait()
        at = pl.ds(i * part_k, part_k)
        more = jnp.dot(hidden[:, at], w_in[at, :], preferred_element_type=F32)
        part = more if part is None else part + more
        if i == 0:
            for load in rest[EARLY:]:
                load.start()
    part = part.reshape(T, frames, width)
    ctx_send[...] = part.astype(BF16)
    ctx_own[...] = part
    pl.semaphore_wait(barrier, len(peers_d) + len(peers_p))
    ctx_copies = [
        send(ctx_send.at[p], ctx_recv.at[i], ctx_ss.at[i], ctx_rs.at[i], peers_t[i])
        for i, p in enumerate(places)
    ]

    rest[0].wait()
    rest[1].wait()
    mask_row = mask[...].astype(F32)
    spot = lax.broadcasted_iota(jnp.int32, (frames, nframes), 0) + t * frames
    here = lax.broadcasted_iota(jnp.int32, (frames, nframes), 1)
    mine = spot == here
    tok = tokens[...].astype(F32)
    lanes = lax.broadcasted_iota(jnp.int32, (frames, vocab), 1).astype(F32)
    hot = [
        jnp.sum(jnp.where(mine, tok[k : k + 1, :], 0.0), 1, keepdims=True) == lanes
        for k in range(steps)
    ]
    rest[2].wait()
    prev = jnp.concatenate([jnp.where(h, 1.0, 0.0).astype(BF16) for h in hot[:-1]], 0)
    gath[...] = jnp.dot(prev, embed[...], preferred_element_type=F32)
    mcol = jnp.sum(jnp.where(mine, mask_row, 0.0), 1, keepdims=True)
    rest[3].wait()
    rest[4].wait()
    gvec = gain[...]

    ctx = ctx_own[t]
    for i in range(T - 1):
        got(ctx_copies[i])
        ctx = ctx + ctx_recv[i].astype(F32)
    ctx = ctx.astype(BF16).astype(F32)
    inputs = jnp.concatenate([ctx] * steps, 0) + jnp.concatenate(
        [jnp.zeros((frames, width), F32), gath[...]], 0
    )
    inverse = lax.rsqrt(jnp.mean(inputs * inputs, -1, keepdims=True) + 1e-06)
    normed = inputs * inverse
    flat = (normed * gvec).astype(BF16)
    scaled[...] = flat
    logits = jnp.dot(flat, w_head[...], preferred_element_type=F32)
    top = jnp.max(logits, -1, keepdims=True)
    powers = jnp.exp(logits - top)
    norm = jnp.sum(powers, -1, keepdims=True)
    onehot = jnp.concatenate([jnp.where(h, 1.0, 0.0) for h in hot], 0)
    weights = jnp.concatenate([mcol] * steps, 0)
    grads = ((powers * (1.0 / norm) - onehot) * weights).astype(BF16)
    gl[...] = grads

    chunk = width // DP
    h1, h2 = [], []

    cut = s1.shape[3]

    def along_dp(j, slot, src, dst, ss, rs):
        return pltpu.make_async_remote_copy(
            src_ref=src, dst_ref=dst.at[slot], send_sem=ss.at[j], recv_sem=rs.at[slot],
            device_id={"dp": j}, device_id_type=MESH,
        )

    def tensor_stage(j):
        acc = hs[j, :, s].astype(F32)
        for e in range(1, S):
            got(h1[j * (S - 1) + e - 1])
            acc = acc + r1[j, e - 1].astype(F32)
        s1[j] = acc[:, :, :cut].astype(BF16)
        for i, p in enumerate(places):
            h2.append(
                send(s1.at[j, p], r2.at[j, i], h2_ss.at[j, i], h2_rs.at[j, i], peers_t[i])
            )

        z1[j] = acc[:, :, cut:].astype(BF16)

        @pl.when(a != j)
        def _():
            along_dp(j, lax.rem(j - a + DP, DP) - 1, z1.at[j], rz, z1_ss, z1_rs).start()

    for j0 in range(0, DP, PAIR):
        term = lax.dot_general(
            scaled[:, j0 * chunk : (j0 + PAIR) * chunk], gl[...], (((0,), (0,)), ((), ())),
            preferred_element_type=F32,
        )
        for j in range(j0, j0 + PAIR):
            hs[j] = term[(j - j0) * chunk : (j - j0 + 1) * chunk].astype(BF16).reshape(
                T, S, piece, vocab
            )
            for e in range(1, S):
                h1.append(
                    send(hs.at[j, :, lax.rem(s + e, S)], r1.at[j, e - 1], h1_ss.at[j, e - 1],
                         h1_rs.at[j, e - 1], {"seq": lax.rem(s + e, S)})
                )

    stat1, stat2 = [], []

    def statistics():
        total = top + jnp.log(norm)
        nll = total - jnp.sum(logits * onehot, -1, keepdims=True)
        left = lax.broadcasted_iota(jnp.int32, st1.shape, 1) < st1.shape[1] // 2
        st1[...] = jnp.where(left, jnp.sum(weights * nll), jnp.sum(weights))
        for i, peer in enumerate(peers_p):
            stat1.append(send(st1, st1_r.at[i], st1_ss.at[i], st1_rs.at[i], peer))

    gc_copies = []

    def context_grad():
        grad_scaled = lax.dot_general(
            gl[...], w_head[...], (((1,), (1,)), ((), ())), preferred_element_type=F32
        )
        g = grad_scaled * gvec
        gi = inverse * (g - normed * jnp.mean(g * normed, -1, keepdims=True))
        gsum = gi[0:frames]
        for k in range(1, steps):
            gsum = gsum + gi[k * frames : (k + 1) * frames]
        gc[t] = gsum.astype(BF16)
        for i in range(T - 1):
            gc_copies.append(
                send(gc.at[t], gc.at[t], gc_ss.at[i], gc_rs.at[i], peers_t[i])
            )

    if STAT < 0:
        statistics()
    for j in range(DP):
        tensor_stage(j)
        if j == min(STAT, DP - 1):
            statistics()
        if j == min(GCAT, DP - 1):
            context_grad()

    z2c = []

    def z_stage():
        acc = jnp.zeros(zown.shape, F32)
        for j in range(DP):
            acc = acc + jnp.where(a == j, z1[j].astype(F32), 0.0)
        for d in range(DP - 1):
            along_dp(d, d, z1.at[d], rz, z1_ss, z1_rs).wait_recv()
            acc = acc + rz[d].astype(F32)
        z2[...] = acc.astype(BF16)
        zown[...] = acc
        for i, p in enumerate(places):
            z2c.append(send(z2.at[p], rz2.at[i], z2_ss.at[i], z2_rs.at[i], peers_t[i]))

    for j in range(DP):
        if j == min(LAT, DP - 1):
            stats = st1[...]
            for i in range(len(peers_p)):
                got(stat1[i])
                stats = stats + st1_r[i]
            st2[...] = stats
            for i, peer in enumerate(peers_d):
                stat2.append(send(st2, st2_r.at[i], st2_ss.at[i], st2_rs.at[i], peer))
        acc = s1[j, t].astype(F32)
        for i in range(T - 1):
            got(h2[j * (T - 1) + i])
            acc = acc + r2[j, i].astype(F32)

        @pl.when(a == j)
        def _():
            own[...] = acc

        @pl.when(a != j)
        def _():
            s2[j] = acc.astype(BF16)
            along_dp(j, lax.rem(j - a + DP, DP) - 1, s2.at[j], r3, h3_ss, h3_rs).start()

        if j == min(ZAT, DP - 1):
            z_stage()

    for i in range(DP - 1):
        got(stat2[i])
        stats = stats + st2_r[i]
    half = st1.shape[1] // 2
    share = 1.0 / stats[0:1, half : half + 1]
    for i in range(T - 1):
        got(gc_copies[i])
    product = lax.dot_general(
        gc[...].reshape(nframes, width), w_in[...], (((1,), (1,)), ((), ())),
        preferred_element_type=F32,
    )
    gh_o[...] = (product * share).astype(BF16)
    loss_o[...] = stats * share

    groups = vocab // 128
    low = cut // 128
    acc = zown[t]
    for i in range(T - 1):
        got(z2c[i])
        acc = acc + rz2[i].astype(F32)
    acc = acc * share
    for b in range(low, groups):
        head_o[pl.ds(b, piece, stride=groups), :] = acc[:, (b - low) * 128 : (b - low + 1) * 128]
    acc = own[...]
    for d in range(DP - 1):
        along_dp(d, d, s2.at[d], r3, h3_ss, h3_rs).wait_recv()
        acc = acc + r3[d].astype(F32)
    acc = acc * share
    for b in range(low):
        head_o[pl.ds(b, piece, stride=groups), :] = acc[:, b * 128 : (b + 1) * 128]
    for copy in sends:
        copy.wait_send()
    for j in range(DP):

        @pl.when(a != j)
        def _():
            along_dp(j, 0, z1.at[j], rz, z1_ss, z1_rs).wait_send()
            along_dp(j, 0, s2.at[j], r3, h3_ss, h3_rs).wait_send()


def write_out(loss_i, head_i, gh_i, loss_o, head_o, gh_o, loss_v, sem):
    copies = [
        pltpu.make_async_copy(src, dst, sem.at[i])
        for i, (src, dst) in enumerate([(gh_i, gh_o), (head_i, head_o), (loss_v, loss_o)])
    ]
    copies[0].start()
    copies[1].start()
    loss_v[...] = loss_i[0:1, 0:1]
    copies[2].start()
    for copy in copies:
        copy.wait()


def per_device_kernel(hidden, w_in, embed, gain, w_head, tokens, frame_mask):
    DP, T, S = lax.axis_size("dp"), lax.axis_size("tensor"), lax.axis_size("seq")
    nframes, feats = hidden.shape
    steps = tokens.shape[1]
    frames = nframes // T
    width, vocab = w_head.shape
    rows = frames * steps
    piece = width // (DP * T * S)
    tail = max(vocab // 128 * ZSHARE // 8, 1) * 128
    cut = vocab - tail
    V = pltpu.VMEM
    dma = pltpu.SemaphoreType.DMA
    scratch = [
        V(hidden.shape, BF16), V(w_in.shape, BF16), V(embed.shape, BF16), V((1, width), F32),
        V(w_head.shape, BF16), V((steps, nframes), jnp.int32), V((1, nframes), jnp.int32),
        V((T, frames, width), F32),
        V((T, frames, width), BF16),
        V((T - 1, frames, width), BF16),
        V((rows - frames, width), F32),
        V((rows, width), BF16),
        V((rows, vocab), BF16),
        V((DP, T, S, piece, vocab), BF16),
        V((DP, S - 1, T, piece, vocab), BF16),
        V((DP, T, piece, cut), BF16),
        V((DP, T - 1, piece, cut), BF16),
        V((DP, piece, cut), BF16),
        V((DP - 1, piece, cut), BF16),
        V((piece, cut), F32),
        V((DP, T, piece, tail), BF16),
        V((DP - 1, T, piece, tail), BF16),
        V((T, piece, tail), F32),
        V((T, piece, tail), BF16),
        V((T - 1, piece, tail), BF16),
        V((T, frames, width), BF16),
        V((8, 128), F32), V((T * S - 1, 8, 128), F32),
        V((8, 128), F32), V((DP - 1, 8, 128), F32),
        dma((2 * KCH + 5,)),
        dma((T - 1,)), dma((T - 1,)), dma((T - 1,)), dma((T - 1,)),
        dma((DP, S - 1)), dma((DP, S - 1)), dma((DP, T - 1)), dma((DP, T - 1)),
        dma((DP,)), dma((DP - 1,)), dma((DP,)), dma((DP - 1,)), dma((T - 1,)), dma((T - 1,)),
        dma((T * S - 1,)), dma((T * S - 1,)), dma((DP - 1,)), dma((DP - 1,)),
    ]
    head_shape = jax.ShapeDtypeStruct((piece * vocab // 128, 128), F32)
    gh_shape = jax.ShapeDtypeStruct((nframes, feats), BF16)
    vmem = pl.BlockSpec(memory_space=pltpu.VMEM)
    results = pl.pallas_call(
        functools.partial(kernel, (DP, T, S)),
        out_shape=(jax.ShapeDtypeStruct((8, 128), F32), head_shape, gh_shape),
        in_specs=[pl.BlockSpec(memory_space=pltpu.HBM)] * 7,
        out_specs=(vmem, vmem, vmem),
        scratch_shapes=scratch,
        compiler_params=pltpu.CompilerParams(
            collective_id=0, has_side_effects=True, vmem_limit_bytes=40 << 20
        ),
        name="decode",
    )(*[pltpu.with_memory_space_constraint(x, pltpu.HBM) for x in (hidden, w_in, embed, gain.reshape(1, -1), w_head, tokens.T, frame_mask.reshape(1, -1))])
    loss, head, grad_hidden = pl.pallas_call(
        write_out,
        out_shape=(jax.ShapeDtypeStruct((1, 1), F32), head_shape, gh_shape),
        in_specs=[vmem] + [pl.BlockSpec(memory_space=pl.ANY)] * 2,
        out_specs=(pl.BlockSpec(memory_space=pltpu.HBM),) * 3,
        scratch_shapes=[V((1, 1), F32), dma((3,))],
        compiler_params=pltpu.CompilerParams(vmem_limit_bytes=4 << 20),
        name="write_out",
    )(*results)
    return loss.reshape(()), head.reshape(-1), grad_hidden


def solution(mesh):
    def per_device(hidden, w_in, embed, gain, w_head, tokens, frame_mask):
        DP, T, S = mesh.shape["dp"], mesh.shape["tensor"], mesh.shape["seq"]
        width, vocab = w_head.shape
        fits = (
            width % (16 * DP * T * S) == 0
            and width % (128 * DP) == 0
            and vocab % 128 == 0
            and vocab > 128
            and hidden.shape[0] % (16 * T) == 0
            and min(DP, T, S) > 1
            and DP % PAIR == 0
        )
        run = per_device_kernel if fits else per_device_plain
        return run(hidden, w_in, embed, gain, w_head, tokens, frame_mask)

    placed = (
        P(("dp", "seq"), "tensor"),
        P("tensor", None),
        P(),
        P(),
        P(),
        P(("dp", "seq"), None),
        P(("dp", "seq")),
    )
    return jax.shard_map(
        per_device,
        mesh=mesh,
        in_specs=placed,
        out_specs=(P(), P(("dp", "tensor", "seq")), P(("dp", "seq"), "tensor")),
        check_vma=False,
    )
```

```python
import functools

import jax
import jax.numpy as jnp
from jax import lax
from jax.experimental import pallas as pl
from jax.experimental.pallas import tpu as pltpu
from jax.sharding import PartitionSpec as P

F32 = jnp.float32
BF16 = jnp.bfloat16
MESH = pl.DeviceIdType.MESH
KCH = 2
ORDER = ("T0", "T1", "T2", "T3", "J", "L", "K0", "K1", "Z", "K2", "K3", "S", "M")
ZSHARE = 2
EARLY = 7


def decode_terms(context, tok_rows, mask_rows, embed, gain, w_head, count_fn):
    frames = context.shape[0]
    width = context.shape[1]
    steps = tok_rows.shape[1]
    before = embed[tok_rows[:, :-1]].astype(jnp.float32)
    leading = jnp.zeros((frames, 1, width), jnp.float32)
    inputs = context.astype(jnp.float32)[:, None, :] + jnp.concatenate([leading, before], 1)
    inverse = lax.rsqrt(jnp.mean(inputs * inputs, -1, keepdims=True) + 1e-06)
    normed = inputs * inverse
    scaled = (normed * gain).astype(jnp.bfloat16)
    flat = scaled.reshape(frames * steps, width)
    logits = jnp.dot(flat, w_head, preferred_element_type=jnp.float32)
    top = jnp.max(logits, -1, keepdims=True)
    total = top[:, 0] + jnp.log(jnp.sum(jnp.exp(logits - top), -1))
    target = tok_rows.reshape(-1)
    onehot = (target[:, None] == jnp.arange(w_head.shape[1], dtype=jnp.int32)[None, :]).astype(
        jnp.float32
    )
    nll = total - jnp.sum(logits * onehot, -1)
    weights = (mask_rows.astype(jnp.float32)[:, None] * jnp.ones((1, steps), jnp.float32)).reshape(
        -1
    )
    count, loss_sum = count_fn(
        steps * jnp.sum(mask_rows.astype(jnp.float32)), jnp.sum(weights * nll)
    )
    probs = jnp.exp(logits - total[:, None])
    grad_logits = ((probs - onehot) * weights[:, None] / count).astype(jnp.bfloat16)
    head_term = lax.dot_general(
        flat, grad_logits, (((0,), (0,)), ((), ())), preferred_element_type=jnp.float32
    )
    grad_scaled = lax.dot_general(
        grad_logits, w_head, (((1,), (1,)), ((), ())), preferred_element_type=jnp.float32
    )
    scaled_grad = grad_scaled.reshape(inputs.shape) * gain
    grad_inputs = inverse * (
        scaled_grad - normed * jnp.mean(scaled_grad * normed, -1, keepdims=True)
    )
    grad_context = jnp.sum(grad_inputs, 1).astype(jnp.bfloat16)
    return (loss_sum / count, head_term, grad_context)


def add_totals(count_local, loss_local):
    return lax.psum((count_local, loss_local), ("dp", "tensor", "seq"))


def per_device_plain(hidden, w_in, embed, gain, w_head, tokens, frame_mask):
    groups = lax.axis_size("tensor")
    rows = hidden.shape[0] // groups
    context = lax.psum_scatter(
        jnp.dot(hidden, w_in, preferred_element_type=jnp.float32),
        "tensor",
        scatter_dimension=0,
        tiled=True,
    ).astype(jnp.bfloat16)
    offset = lax.axis_index("tensor") * rows
    tok_rows = lax.dynamic_slice_in_dim(tokens, offset, rows, 0)
    mask_rows = lax.dynamic_slice_in_dim(frame_mask, offset, rows, 0)
    loss, head_term, grad_context = decode_terms(
        context, tok_rows, mask_rows, embed, gain, w_head, add_totals
    )
    flat_term = head_term.reshape(-1)
    partial_grad = lax.psum_scatter(
        flat_term.astype(jnp.bfloat16), "dp", scatter_dimension=0, tiled=True
    ).astype(jnp.float32)
    grad_head = lax.psum_scatter(partial_grad, ("tensor", "seq"), scatter_dimension=0, tiled=True)
    product = lax.dot_general(
        lax.all_gather(grad_context, "tensor", axis=0, tiled=True),
        w_in,
        (((1,), (1,)), ((), ())),
        preferred_element_type=jnp.float32,
    )
    grad_hidden = product.astype(jnp.bfloat16)
    return (loss, grad_head, grad_hidden)


def kernel(
    sizes, hidden_h, w_in_h, embed_h, gain_h, w_head_h, tokens_h, mask_h,
    loss_o, head_o, gh_o,
    hidden, w_in, embed, gain, w_head, tokens, mask,
    ctx_own, ctx_send, ctx_recv, gath, scaled, gl, hs, r1, s1, r2, s2, r3, own,
    z1, rz, zown, z2, rz2, gc, st1, st1_r, st2, st2_r,
    in_sem, ctx_ss, ctx_rs, gc_ss, gc_rs,
    h1_ss, h1_rs, h2_ss, h2_rs, h3_ss, h3_rs, z1_ss, z1_rs, z2_ss, z2_rs,
    st1_ss, st1_rs, st2_ss, st2_rs, above, below,
):
    DP, T, S = sizes
    a, t, s = lax.axis_index("dp"), lax.axis_index("tensor"), lax.axis_index("seq")
    steps, nframes = tokens.shape
    frames = nframes // T
    width, vocab = w_head.shape
    rows = frames * steps
    piece = width // (DP * T * S)

    TX = 2 if T % 2 == 0 else 1
    TY = T // TX
    ty, tx = t // TX, lax.rem(t, TX)
    moves = sorted(
        [(dy, dx) for dy in range(TY) for dx in range(TX) if dy or dx],
        key=lambda m: -(m[0] > 0) - (m[1] > 0),
    )
    places = [lax.rem(ty + dy, TY) * TX + lax.rem(tx + dx, TX) for dy, dx in moves]

    barrier = pltpu.get_barrier_semaphore()
    peers_t = [{"tensor": p} for p in places]
    peers_p = [
        {"tensor": lax.rem(t + d, T), "seq": lax.rem(s + e, S)}
        for d in range(T)
        for e in range(S)
        if d or e
    ]
    peers_d = [{"dp": lax.rem(a + d, DP)} for d in range(1, DP)]
    for peer in peers_p:
        pl.semaphore_signal(barrier, inc=1, device_id=peer, device_id_type=MESH)

    @pl.when(a > 0)
    def _():
        pl.semaphore_signal(barrier, inc=1, device_id={"dp": a - 1}, device_id_type=MESH)

    @pl.when(a < DP - 1)
    def _():
        pl.semaphore_signal(barrier, inc=1, device_id={"dp": a + 1}, device_id_type=MESH)


    K = KCH
    part_n = width // K
    pairs = [(hidden_h, hidden)]
    for i in range(K):
        at = pl.ds(i * part_n, part_n)
        pairs.append((w_in_h.at[:, at], w_in.at[:, at]))
    pairs += [
        (tokens_h, tokens),
        (mask_h, mask),
        (embed_h, embed),
        (gain_h, gain),
        (w_head_h, w_head),
    ]
    loads = [
        pltpu.make_async_copy(src, dst, in_sem.at[i]) for i, (src, dst) in enumerate(pairs)
    ]
    rest = loads[K + 1 :]
    for load in loads[: K + 1] + rest[:EARLY]:
        load.start()

    sends = []

    def got(copy):
        copy.wait_recv()

    def send(src, dst, ss, rs, peer):
        copy = pltpu.make_async_remote_copy(
            src_ref=src, dst_ref=dst, send_sem=ss, recv_sem=rs, device_id=peer, device_id_type=MESH
        )
        copy.start()
        sends.append(copy)
        return copy

    beside = jnp.where(a > 0, 1, 0) + jnp.where(a < DP - 1, 1, 0)
    loads[0].wait()
    ctx_copies = []
    for n in range(K):
        loads[1 + n].wait()
        at = pl.ds(n * part_n, part_n)
        part = jnp.dot(hidden[...], w_in[:, at], preferred_element_type=F32)
        part = part.reshape(T, frames, part_n)
        ctx_send[n] = part.astype(BF16)
        ctx_own[n] = part
        if n == 0:
            pl.semaphore_wait(barrier, len(peers_p) + beside)
        for i, p in enumerate(places):
            ctx_copies.append(
                send(ctx_send.at[n, p], ctx_recv.at[n, i], ctx_ss.at[n, i], ctx_rs.at[n, i],
                     peers_t[i])
            )

    rest[0].wait()
    rest[1].wait()
    mask_row = mask[...].astype(F32)
    spot = lax.broadcasted_iota(jnp.int32, (frames, nframes), 0) + t * frames
    here = lax.broadcasted_iota(jnp.int32, (frames, nframes), 1)
    mine = spot == here
    tok = tokens[...].astype(F32)
    lanes = lax.broadcasted_iota(jnp.int32, (frames, vocab), 1).astype(F32)
    hot = [
        jnp.sum(jnp.where(mine, tok[k : k + 1, :], 0.0), 1, keepdims=True) == lanes
        for k in range(steps)
    ]
    rest[2].wait()
    prev = jnp.concatenate([jnp.where(h, 1.0, 0.0).astype(BF16) for h in hot[:-1]], 0)
    gath[...] = jnp.dot(prev, embed[...], preferred_element_type=F32)
    mcol = jnp.sum(jnp.where(mine, mask_row, 0.0), 1, keepdims=True)
    rest[3].wait()
    rest[4].wait()
    gvec = gain[...]

    for k in range(DP - 2, 0, -1):

        @pl.when(a == k)
        def _():
            if k < DP - 2:
                pl.semaphore_wait(above, 1)
            pl.semaphore_signal(above, inc=1, device_id={"dp": k - 1}, device_id_type=MESH)
            if k > 1:
                pl.semaphore_wait(below, 1)
            pl.semaphore_signal(below, inc=1, device_id={"dp": k + 1}, device_id_type=MESH)

    halves = []
    for n in range(K):
        ctx = ctx_own[n, t]
        for i in range(T - 1):
            got(ctx_copies[n * (T - 1) + i])
            ctx = ctx + ctx_recv[n, i].astype(F32)
        halves.append(ctx)
    ctx = jnp.concatenate(halves, 1)
    ctx = ctx.astype(BF16).astype(F32)
    @pl.when(a == 0)
    def _():
        pl.semaphore_wait(above, 1)

    @pl.when(a == DP - 1)
    def _():
        pl.semaphore_wait(below, 1)

    inputs = jnp.concatenate([ctx] * steps, 0) + jnp.concatenate(
        [jnp.zeros((frames, width), F32), gath[...]], 0
    )
    inverse = lax.rsqrt(jnp.mean(inputs * inputs, -1, keepdims=True) + 1e-06)
    normed = inputs * inverse
    flat = (normed * gvec).astype(BF16)
    scaled[...] = flat
    logits = jnp.dot(flat, w_head[...], preferred_element_type=F32)
    top = jnp.max(logits, -1, keepdims=True)
    powers = jnp.exp(logits - top)
    norm = jnp.sum(powers, -1, keepdims=True)
    onehot = jnp.concatenate([jnp.where(h, 1.0, 0.0) for h in hot], 0)
    weights = jnp.concatenate([mcol] * steps, 0)
    grads = ((powers * (1.0 / norm) - onehot) * weights).astype(BF16)
    gl[...] = grads

    chunk = width // DP
    h1, h2 = [], []

    cut = s1.shape[3]

    def along_dp(j, slot, src, dst, ss, rs):
        return pltpu.make_async_remote_copy(
            src_ref=src, dst_ref=dst.at[slot], send_sem=ss.at[j], recv_sem=rs.at[slot],
            device_id={"dp": j}, device_id_type=MESH,
        )

    def tensor_stage(j):
        acc = hs[j, :, s].astype(F32)
        for e in range(1, S):
            got(h1[j * (S - 1) + e - 1])
            acc = acc + r1[j, e - 1].astype(F32)
        s1[j] = acc[:, :, :cut].astype(BF16)
        for i, p in enumerate(places):
            h2.append(
                send(s1.at[j, p], r2.at[j, i], h2_ss.at[j, i], h2_rs.at[j, i], peers_t[i])
            )

        z1[j] = acc[:, :, cut:].astype(BF16)

        @pl.when(a != j)
        def _():
            along_dp(j, lax.rem(j - a + DP, DP) - 1, z1.at[j], rz, z1_ss, z1_rs).start()

    term = lax.dot_general(
        scaled[...], gl[...], (((0,), (0,)), ((), ())), preferred_element_type=F32
    )
    hs[...] = term.astype(BF16).reshape(DP, T, S, piece, vocab)
    for j in range(DP):
        for e in range(1, S):
            h1.append(
                send(hs.at[j, :, lax.rem(s + e, S)], r1.at[j, e - 1], h1_ss.at[j, e - 1],
                     h1_rs.at[j, e - 1], {"seq": lax.rem(s + e, S)})
            )
    total = top + jnp.log(norm)
    nll = total - jnp.sum(logits * onehot, -1, keepdims=True)
    left = lax.broadcasted_iota(jnp.int32, st1.shape, 1) < st1.shape[1] // 2
    st1[...] = jnp.where(left, jnp.sum(weights * nll), jnp.sum(weights))
    stat1 = [
        send(st1, st1_r.at[i], st1_ss.at[i], st1_rs.at[i], peer) for i, peer in enumerate(peers_p)
    ]
    stat2 = []

    gc_copies = []

    def context_grad():
        grad_scaled = lax.dot_general(
            gl[...], w_head[...], (((1,), (1,)), ((), ())), preferred_element_type=F32
        )
        g = grad_scaled * gvec
        gi = inverse * (g - normed * jnp.mean(g * normed, -1, keepdims=True))
        gsum = gi[0:frames]
        for k in range(1, steps):
            gsum = gsum + gi[k * frames : (k + 1) * frames]
        gc[t] = gsum.astype(BF16)
        for i in range(T - 1):
            gc_copies.append(
                send(gc.at[t], gc.at[t], gc_ss.at[i], gc_rs.at[i], peers_t[i])
            )

    z2c = []

    def z_stage():
        acc = jnp.zeros(zown.shape, F32)
        for j in range(DP):
            acc = acc + jnp.where(a == j, z1[j].astype(F32), 0.0)
        for d in range(DP - 1):
            along_dp(d, d, z1.at[d], rz, z1_ss, z1_rs).wait_recv()
            acc = acc + rz[d].astype(F32)
        z2[...] = acc.astype(BF16)
        zown[...] = acc
        for i, p in enumerate(places):
            z2c.append(send(z2.at[p], rz2.at[i], z2_ss.at[i], z2_rs.at[i], peers_t[i]))

    def dp_stage(j):
        acc = s1[j, t].astype(F32)
        for i in range(T - 1):
            got(h2[j * (T - 1) + i])
            acc = acc + r2[j, i].astype(F32)

        @pl.when(a == j)
        def _():
            own[...] = acc

        @pl.when(a != j)
        def _():
            s2[j] = acc.astype(BF16)
            along_dp(j, lax.rem(j - a + DP, DP) - 1, s2.at[j], r3, h3_ss, h3_rs).start()

    def statistics():
        stats = st1[...]
        for i in range(len(peers_p)):
            got(stat1[i])
            stats = stats + st1_r[i]
        st2[...] = stats
        for i, peer in enumerate(peers_d):
            stat2.append(send(st2, st2_r.at[i], st2_ss.at[i], st2_rs.at[i], peer))

    scale = []

    def shares():
        stats = st2[...]
        for i in range(DP - 1):
            got(stat2[i])
            stats = stats + st2_r[i]
        half = st1.shape[1] // 2
        scale.append(1.0 / stats[0:1, half : half + 1])
        loss_o[...] = stats * scale[0]

    def hidden_grad():
        for i in range(T - 1):
            got(gc_copies[i])
        product = lax.dot_general(
            gc[...].reshape(nframes, width), w_in[...], (((1,), (1,)), ((), ())),
            preferred_element_type=F32,
        )
        gh_o[...] = (product * scale[0]).astype(BF16)

    plain = dict(J=context_grad, L=statistics, S=shares, M=hidden_grad, Z=z_stage)
    for item in ORDER:
        if item in plain:
            plain[item]()
        else:
            dict(T=tensor_stage, K=dp_stage)[item[0]](int(item[1:]))
    share = scale[0]

    groups = vocab // 128
    low = cut // 128
    acc = zown[t]
    for i in range(T - 1):
        got(z2c[i])
        acc = acc + rz2[i].astype(F32)
    acc = acc * share
    for b in range(low, groups):
        head_o[pl.ds(b, piece, stride=groups), :] = acc[:, (b - low) * 128 : (b - low + 1) * 128]
    acc = own[...]
    for d in range(DP - 1):
        along_dp(d, d, s2.at[d], r3, h3_ss, h3_rs).wait_recv()
        acc = acc + r3[d].astype(F32)
    acc = acc * share
    for b in range(low):
        head_o[pl.ds(b, piece, stride=groups), :] = acc[:, b * 128 : (b + 1) * 128]
    for copy in sends:
        copy.wait_send()
    for j in range(DP):

        @pl.when(a != j)
        def _():
            along_dp(j, 0, z1.at[j], rz, z1_ss, z1_rs).wait_send()
            along_dp(j, 0, s2.at[j], r3, h3_ss, h3_rs).wait_send()


def write_out(loss_i, head_i, gh_i, loss_o, head_o, gh_o, loss_v, sem):
    copies = [
        pltpu.make_async_copy(src, dst, sem.at[i])
        for i, (src, dst) in enumerate([(gh_i, gh_o), (head_i, head_o), (loss_v, loss_o)])
    ]
    copies[0].start()
    copies[1].start()
    loss_v[...] = loss_i[0:1, 0:1]
    copies[2].start()
    for copy in copies:
        copy.wait()


def per_device_kernel(hidden, w_in, embed, gain, w_head, tokens, frame_mask):
    DP, T, S = lax.axis_size("dp"), lax.axis_size("tensor"), lax.axis_size("seq")
    nframes, feats = hidden.shape
    steps = tokens.shape[1]
    frames = nframes // T
    width, vocab = w_head.shape
    rows = frames * steps
    piece = width // (DP * T * S)
    tail = max(vocab // 128 * ZSHARE // 8, 1) * 128
    cut = vocab - tail
    V = pltpu.VMEM
    dma = pltpu.SemaphoreType.DMA
    scratch = [
        V(hidden.shape, BF16), V(w_in.shape, BF16), V(embed.shape, BF16), V((1, width), F32),
        V(w_head.shape, BF16), V((steps, nframes), jnp.int32), V((1, nframes), jnp.int32),
        V((KCH, T, frames, width // KCH), F32),
        V((KCH, T, frames, width // KCH), BF16),
        V((KCH, T - 1, frames, width // KCH), BF16),
        V((rows - frames, width), F32),
        V((rows, width), BF16),
        V((rows, vocab), BF16),
        V((DP, T, S, piece, vocab), BF16),
        V((DP, S - 1, T, piece, vocab), BF16),
        V((DP, T, piece, cut), BF16),
        V((DP, T - 1, piece, cut), BF16),
        V((DP, piece, cut), BF16),
        V((DP - 1, piece, cut), BF16),
        V((piece, cut), F32),
        V((DP, T, piece, tail), BF16),
        V((DP - 1, T, piece, tail), BF16),
        V((T, piece, tail), F32),
        V((T, piece, tail), BF16),
        V((T - 1, piece, tail), BF16),
        V((T, frames, width), BF16),
        V((8, 128), F32), V((T * S - 1, 8, 128), F32),
        V((8, 128), F32), V((DP - 1, 8, 128), F32),
        dma((KCH + 6,)),
        dma((KCH, T - 1)), dma((KCH, T - 1)), dma((T - 1,)), dma((T - 1,)),
        dma((DP, S - 1)), dma((DP, S - 1)), dma((DP, T - 1)), dma((DP, T - 1)),
        dma((DP,)), dma((DP - 1,)), dma((DP,)), dma((DP - 1,)), dma((T - 1,)), dma((T - 1,)),
        dma((T * S - 1,)), dma((T * S - 1,)), dma((DP - 1,)), dma((DP - 1,)),
        pltpu.SemaphoreType.REGULAR, pltpu.SemaphoreType.REGULAR,
    ]
    head_shape = jax.ShapeDtypeStruct((piece * vocab // 128, 128), F32)
    gh_shape = jax.ShapeDtypeStruct((nframes, feats), BF16)
    vmem = pl.BlockSpec(memory_space=pltpu.VMEM)
    results = pl.pallas_call(
        functools.partial(kernel, (DP, T, S)),
        out_shape=(jax.ShapeDtypeStruct((8, 128), F32), head_shape, gh_shape),
        in_specs=[pl.BlockSpec(memory_space=pltpu.HBM)] * 7,
        out_specs=(vmem, vmem, vmem),
        scratch_shapes=scratch,
        compiler_params=pltpu.CompilerParams(
            collective_id=0, has_side_effects=True, vmem_limit_bytes=40 << 20
        ),
        name="decode",
    )(*[pltpu.with_memory_space_constraint(x, pltpu.HBM) for x in (hidden, w_in, embed, gain.reshape(1, -1), w_head, tokens.T, frame_mask.reshape(1, -1))])
    loss, head, grad_hidden = pl.pallas_call(
        write_out,
        out_shape=(jax.ShapeDtypeStruct((1, 1), F32), head_shape, gh_shape),
        in_specs=[vmem] + [pl.BlockSpec(memory_space=pl.ANY)] * 2,
        out_specs=(pl.BlockSpec(memory_space=pltpu.HBM),) * 3,
        scratch_shapes=[V((1, 1), F32), dma((3,))],
        compiler_params=pltpu.CompilerParams(vmem_limit_bytes=4 << 20),
        name="write_out",
    )(*results)
    return loss.reshape(()), head.reshape(-1), grad_hidden


def solution(mesh):
    def per_device(hidden, w_in, embed, gain, w_head, tokens, frame_mask):
        DP, T, S = mesh.shape["dp"], mesh.shape["tensor"], mesh.shape["seq"]
        width, vocab = w_head.shape
        fits = (
            width % (16 * DP * T * S) == 0
            and width % (128 * DP) == 0
            and width % (128 * KCH) == 0
            and vocab % 128 == 0
            and vocab > 128
            and hidden.shape[0] % (16 * T) == 0
            and min(DP, T, S) > 1
            and DP == 4
        )
        run = per_device_kernel if fits else per_device_plain
        return run(hidden, w_in, embed, gain, w_head, tokens, frame_mask)

    placed = (
        P(("dp", "seq"), "tensor"),
        P("tensor", None),
        P(),
        P(),
        P(),
        P(("dp", "seq"), None),
        P(("dp", "seq")),
    )
    return jax.shard_map(
        per_device,
        mesh=mesh,
        in_specs=placed,
        out_specs=(P(), P(("dp", "tensor", "seq")), P(("dp", "seq"), "tensor")),
        check_vma=False,
    )
```
